32 devices in a mesh: sect: 2 (over core), lang: 4 (over z), mp: 4 (over y, x).
Axes of the slice: x: 2, y: 2, z: 4, core: 2. Of those that a mesh axis runs over, the one named last changes fastest.
Arguments:
- memory: bfloat16 [4, 2, 128, 4096], P('lang', None, None, ('sect', 'mp')), may hold values from -6 to 6
- queries: bfloat16 [4, 4, 128, 3072], P('lang', 'sect', None, 'mp'), may hold values from -6 to 6
- out_grad: bfloat16 [4, 4, 128, 3072], P('lang', 'sect', None, 'mp'), may hold values from -6 to 6
- key_weight: bfloat16 [4, 4096, 3072], P('lang', None, 'mp'), may hold values from -0.09375 to 0.09375
- value_weight: bfloat16 [4, 4096, 3072], P('lang', None, 'mp'), may hold values from -0.09375 to 0.09375
- lang_rows: int32 [4, 4], P('lang'), may hold values from 0 to 128, as said below
- group_of_lang: int32 [4], replicated, may hold values from 0 to 3, each once
- src_len: int32 [4, 2], P('lang'), may hold values from 16 to 128
Outputs:
- mem_grad: bfloat16 [4, 2, 128, 4096], P('lang', None, None, ('sect', 'mp'))
The draws below stay inside these ranges and needn't reach their ends.
Inputs may be any that keep to these rules, and one draw needn't show every extreme that they name: `lang_rows`: each entry is 0 or 128; each row has exactly 2 nonzero entries.
All inputs are finite; a program needn't handle non-finite values.
Results may differ from the reference program's by a relative error of at most 0.013.
Values may be sent and summed in bfloat16 or wider, within the bound.
A program may use at most 128 MiB of HBM per device.

```python
import jax
import jax.numpy as jnp
from jax import lax

D = 4096
HEADS = 24
HD = 128
SRC_LEN = 128
TGT = 128
TARGET_LANGUAGES = 4
BLK_DEV = 2
N_LANG = 4


def draw_lang_rows(key, part):
    key_heavy, key_first, key_noise = jax.random.split(key, 3)
    busiest_language = jax.random.randint(key_heavy, (TARGET_LANGUAGES,), 0, 4)
    leading_language = jax.random.randint(key_first, (), 0, TARGET_LANGUAGES)
    random_noise = jax.random.randint(key_noise, (TARGET_LANGUAGES, TARGET_LANGUAGES), 0, 65536)
    language_index = jnp.arange(TARGET_LANGUAGES, dtype=jnp.int32)
    extra_score = jnp.where(language_index == leading_language, 8 * 65536, 0) + busiest_language * 65536
    score_table = (random_noise + extra_score[None, :]) * TARGET_LANGUAGES + language_index[None, :]
    picked_values, top_index = lax.top_k(score_table, BLK_DEV)
    chosen = jnp.sum((top_index[:, :, None] == language_index[None, None, :]).astype(jnp.int32), axis=1)
    return (chosen * SRC_LEN).astype(jnp.int32)


def draw_src_len(key, part):
    key_base, key_spot = jax.random.split(jax.random.fold_in(key, 7))
    base_len = jax.random.randint(key_base, (TARGET_LANGUAGES, BLK_DEV), SRC_LEN // 8, SRC_LEN + 1)
    spot_index = jax.random.randint(key_spot, (), 0, TARGET_LANGUAGES * BLK_DEV)
    flat_index = jnp.arange(TARGET_LANGUAGES * BLK_DEV, dtype=jnp.int32).reshape(TARGET_LANGUAGES, BLK_DEV)
    return jnp.where(flat_index == spot_index, SRC_LEN, base_len).astype(jnp.int32)


def block_levels(rng, shape, cuts, smallest, largest):
    gain, own = 1.0, jax.random.fold_in(rng, 6)
    for axis_at, blocks in cuts:
        heights = jnp.exp(jax.random.uniform(jax.random.fold_in(own, axis_at), (blocks,), jnp.float32, smallest / len(cuts), largest / len(cuts)))
        gain = gain * jnp.repeat(heights, shape[axis_at] // blocks).reshape([-1 if axis == axis_at else 1 for axis in range(len(shape))])
    return gain


def scatter_about(own_key, extent, spread, limit, cuts=(), held_as=jnp.bfloat16):
    entries = jax.random.normal(own_key, extent, jnp.float32) * spread
    if len(cuts) > 0:
        entries = block_levels(own_key, extent, cuts, -0.22, 0.18) * entries
    return jnp.clip(entries, min=-limit, max=limit).astype(held_as)


def setup_inputs(seed: int = 0) -> dict:
    key_list = jax.random.split(jax.random.key(seed), 9)
    memory = scatter_about(key_list[0], (N_LANG, BLK_DEV, SRC_LEN, D), 1.0, 6.0, ((0, 4), (3, 8)))
    queries = scatter_about(key_list[1], (N_LANG, N_LANG, TGT, HEADS * HD), 1.0, 6.0, ((0, 4), (1, 2), (3, 4)))
    out_grad = scatter_about(key_list[2], (N_LANG, N_LANG, TGT, HEADS * HD), 1.0, 6.0, ((0, 4), (1, 2), (3, 4)))
    key_weight = scatter_about(key_list[3], (N_LANG, D, HEADS * HD), D ** -0.5, 0.09375, ((0, 4), (2, 4)))
    value_weight = scatter_about(key_list[4], (N_LANG, D, HEADS * HD), D ** -0.5, 0.09375, ((0, 4), (2, 4)))
    lang_rows = draw_lang_rows(jax.random.fold_in(key_list[8], 71), 0)
    group_of_lang = jax.random.permutation(key_list[6], TARGET_LANGUAGES).astype(jnp.int32)
    src_len = draw_src_len(jax.random.fold_in(key_list[8], 71), 0)
    return dict(memory=memory, queries=queries, out_grad=out_grad, key_weight=key_weight, value_weight=value_weight, lang_rows=lang_rows, group_of_lang=group_of_lang, src_len=src_len)


def key_grads(key_rows, value_rows, queries, out_grad, lengths, head_dim):
    slots, source, width = key_rows.shape
    target = queries.shape[1]
    heads = width // head_dim
    key_four = key_rows.reshape(slots, source, heads, head_dim).astype(jnp.float32)
    value_four = value_rows.reshape(slots, source, heads, head_dim).astype(jnp.float32)
    query_four = queries.reshape(slots, target, heads, head_dim).astype(jnp.float32)
    grad_four = out_grad.reshape(slots, target, heads, head_dim).astype(jnp.float32)
    scaling = head_dim ** -0.5
    score_table = jnp.einsum("sqhd,skhd->shqk", query_four, key_four) * scaling
    visible = jnp.arange(source, dtype=jnp.int32)[None, :] < lengths[:, None]
    weights = jnp.where(visible[:, None, None, :], jnp.exp(score_table), 0.0)
    probs = weights / jnp.sum(weights, axis=-1, keepdims=True)
    probs_low = probs.astype(jnp.bfloat16)
    grad_probs = jnp.einsum("sqhd,skhd->shqk", grad_four, value_four)
    deltas = jnp.sum(probs * grad_probs, axis=-1, keepdims=True)
    grad_scores = (probs * (grad_probs - deltas) * scaling).astype(jnp.bfloat16)
    grad_keys = jnp.einsum("shqk,sqhd->skhd", grad_scores.astype(jnp.float32), query_four)
    grad_values = jnp.einsum("shqk,sqhd->skhd", probs_low.astype(jnp.float32), grad_four)
    grad_keys = grad_keys.astype(jnp.bfloat16).reshape(slots, source, width)
    grad_values = grad_values.astype(jnp.bfloat16).reshape(slots, source, width)
    return grad_keys, grad_values


def reference(memory, queries, out_grad, key_weight, value_weight, lang_rows, group_of_lang, src_len):
    shards = memory.shape[0]
    blocks = memory.shape[1]
    is_live = (lang_rows > 0).astype(jnp.int32)
    ranking = jnp.cumsum(is_live, axis=1) - 1
    block_index = jnp.arange(blocks, dtype=jnp.int32)
    chosen = (is_live[:, None, :] > 0) & (ranking[:, None, :] == block_index[None, :, None])
    language_index = jnp.arange(lang_rows.shape[1], dtype=jnp.int32)
    block_lang = jnp.sum(jnp.where(chosen, language_index[None, None, :], 0), axis=2).astype(jnp.int32)
    block_group = group_of_lang[block_lang].astype(jnp.int32)

    def one_block(flat):
        shard = flat // blocks
        within = flat % blocks
        group = block_group[shard, within]
        panel = memory[shard, within]
        key_rows = jnp.dot(panel, key_weight[group], preferred_element_type=jnp.float32).astype(jnp.bfloat16)
        value_rows = jnp.dot(panel, value_weight[group], preferred_element_type=jnp.float32).astype(jnp.bfloat16)
        grad_keys, grad_values = key_grads(key_rows[None], value_rows[None], queries[group, shard][None], out_grad[group, shard][None], src_len[shard, within][None], HD)
        term = jnp.dot(grad_keys[0], key_weight[group].T, preferred_element_type=jnp.float32)
        term = term + jnp.dot(grad_values[0], value_weight[group].T, preferred_element_type=jnp.float32)
        return term.astype(jnp.bfloat16)

    result = lax.map(one_block, jnp.arange(shards * blocks, dtype=jnp.int32))
    return result.reshape(memory.shape)
```

```python
import functools

import jax
import jax.numpy as jnp
from jax import lax
from jax.experimental import pallas as pl
from jax.experimental.pallas import tpu as pltpu
from jax.sharding import PartitionSpec as P

HD = 128
MESH = pl.DeviceIdType.MESH
NT = (((1,), (1,)), ((), ()))


def kernel(
    dims,
    lang_rows,
    group_of_lang,
    src_len,
    memory,
    queries_hbm,
    grads_hbm,
    key_hbm,
    value_hbm,
    out,
    key_w,
    value_w,
    query_v,
    grad_v,
    outgoing,
    out_len,
    got_len,
    rows,
    acc_k,
    acc_v,
    key_rows,
    value_rows,
    part,
    own,
    inbox,
    reduced,
    arrived,
    load_sem,
    z_send,
    z_len_send,
    len_recv,
    rows_recv,
    mp_send,
    part_send,
    part_recv,
    back_send,
    back_recv,
):
    sectors, groups, quarters, half, blocks, source, eighth, width, heads_w = dims
    ms, ml, mq = lax.axis_index("sect"), lax.axis_index("lang"), lax.axis_index("mp")
    languages = lang_rows.shape[1]

    loads = [
        pltpu.make_async_copy(key_hbm.at[0], key_w, load_sem.at[0]),
        pltpu.make_async_copy(value_hbm.at[0], value_w, load_sem.at[1]),
        pltpu.make_async_copy(queries_hbm.at[0], query_v, load_sem.at[2]),
        pltpu.make_async_copy(grads_hbm.at[0], grad_v, load_sem.at[3]),
    ]

    barrier = pltpu.get_barrier_semaphore()
    for ds in range(sectors):
        for dl in range(groups):
            if ds or dl:
                peer = (lax.rem(ms + ds, sectors), lax.rem(ml + dl, groups), mq)
                pl.semaphore_signal(barrier, inc=1, device_id=peer, device_id_type=MESH)
    for dq in range(1, quarters):
        peer = (ms, ml, lax.rem(mq + dq, quarters))
        pl.semaphore_signal(barrier, inc=1, device_id=peer, device_id_type=MESH)
    for load in loads:
        load.start()

    live, rank, count = [], [], 0
    for c in range(languages):
        live.append((lang_rows[0, c] > 0).astype(jnp.int32))
        rank.append(count)
        count = count + live[c]
    home = lax.div(ml, half)
    slot = lax.rem(ml, half)
    at_home = home == ms
    for dl in range(groups):
        g = lax.rem(ml + dl, groups)
        index, routed = 0, 0
        for c in range(languages):
            hit = jnp.where(group_of_lang[c] == g, live[c], 0)
            index = index + hit * rank[c]
            routed = routed + hit
        outgoing[dl] = memory[0, index]
        length = jnp.maximum(jnp.where(routed > 0, src_len[0, index], 1), 1)
        out_len[dl] = jnp.full(out_len.shape[1:], length, jnp.int32)

    pl.semaphore_wait(barrier, sectors * groups - 1 + quarters - 1)

    def z_copy(dl):
        g = lax.rem(ml + dl, groups)
        data = pltpu.make_async_remote_copy(
            src_ref=outgoing.at[dl],
            dst_ref=rows.at[ms, mq, slot],
            send_sem=z_send.at[dl],
            recv_sem=rows_recv.at[ms, mq, slot],
            device_id=(home, g, mq),
            device_id_type=MESH,
        )
        lens = pltpu.make_async_remote_copy(
            src_ref=out_len.at[dl],
            dst_ref=got_len.at[slot, ms],
            send_sem=z_len_send.at[dl],
            recv_sem=len_recv.at[slot, ms],
            device_id=(home, g, mq),
            device_id_type=MESH,
        )
        return data, lens

    def local_in():
        return (
            pltpu.make_async_copy(
                outgoing.at[0], rows.at[ms, mq, slot], rows_recv.at[ms, mq, slot]
            ),
            pltpu.make_async_copy(
                out_len.at[0], got_len.at[slot, ms], len_recv.at[slot, ms]
            ),
        )

    @pl.when(at_home)
    def _():
        for copy in local_in():
            copy.start()

    @pl.when(jnp.logical_not(at_home))
    def _():
        for copy in z_copy(0):
            copy.start()

    for dl in range(1, groups):
        for copy in z_copy(dl):
            copy.start()

    def landed(s, q, ls):
        view = rows.at[s, q, ls]
        pltpu.make_async_copy(view, view, rows_recv.at[s, q, ls]).wait()

    def mp_copy(s, ls, dq):
        return pltpu.make_async_remote_copy(
            src_ref=rows.at[s, mq, ls],
            dst_ref=rows.at[s, mq, ls],
            send_sem=mp_send.at[dq - 1, s, ls],
            recv_sem=rows_recv.at[s, mq, ls],
            device_id=(ms, ml, lax.rem(mq + dq, quarters)),
            device_id_type=MESH,
        )

    nearest = jnp.clip(ml - ms * half, 0, half - 1)

    def forward(i, carry):
        ls = lax.rem(nearest + lax.div(i, sectors), half)
        s = lax.rem(i, sectors)
        landed(s, mq, ls)
        for dq in range(quarters - 1, 0, -1):
            mp_copy(s, ls, dq).start()
        return carry

    lax.fori_loop(0, sectors * half, forward, 0)

    pair = 2 if half % 2 == 0 else 1
    tall = pair * source
    acc_k[...] = jnp.zeros_like(acc_k)
    acc_v[...] = jnp.zeros_like(acc_v)
    for load in loads:
        load.wait()

    def project(i, carry):
        q = lax.rem(mq + lax.div(i, sectors), quarters)
        s = lax.rem(i, sectors)

        @pl.when(q != mq)
        def _():
            def wait_slot(ls, c):
                landed(s, q, ls)
                return c

            lax.fori_loop(0, half, wait_slot, 0)

        start = pl.multiple_of((s * quarters + q) * eighth, eighth)

        def chunk(m, c):
            x = rows[s, q, pl.ds(m * pair, pair)].reshape(tall, eighth)
            at = pl.ds(pl.multiple_of(m * tall, tall), tall)
            acc_k[at, :] += jnp.dot(
                x, key_w[pl.ds(start, eighth), :], preferred_element_type=jnp.float32
            )
            acc_v[at, :] += jnp.dot(
                x, value_w[pl.ds(start, eighth), :], preferred_element_type=jnp.float32
            )
            return c

        return lax.fori_loop(0, half // pair, chunk, carry)

    lax.fori_loop(0, sectors * quarters, project, 0)

    def wait_len(i, carry):
        ls, s = lax.div(i, sectors), lax.rem(i, sectors)
        view = got_len.at[ls, s]
        pltpu.make_async_copy(view, view, len_recv.at[ls, s]).wait()
        return carry

    lax.fori_loop(0, sectors * half, wait_len, 0)

    scaling = HD ** (-0.5)
    position = lax.broadcasted_iota(jnp.int32, (source, query_v.shape[1]), 0)

    def attend(ls, carry):
        at = pl.ds(pl.multiple_of(ls * source, source), source)
        visible = position < got_len[ls, 0][0:1, :]
        for h in range(heads_w // HD):
            cols = slice(h * HD, (h + 1) * HD)
            k = acc_k[at, cols].astype(jnp.bfloat16)
            v = acc_v[at, cols].astype(jnp.bfloat16)
            q = query_v[ls, :, cols]
            d = grad_v[ls, :, cols]
            scores = lax.dot_general(k, q, NT, preferred_element_type=jnp.float32) * scaling
            weights = jnp.where(visible, jnp.exp(scores), 0.0)
            probs = weights / jnp.sum(weights, axis=0, keepdims=True)
            grad_probs = lax.dot_general(v, d, NT, preferred_element_type=jnp.float32)
            deltas = jnp.sum(probs * grad_probs, axis=0, keepdims=True)
            grad_scores = (probs * (grad_probs - deltas) * scaling).astype(jnp.bfloat16)
            key_rows[at, cols] = jnp.dot(
                grad_scores, q, preferred_element_type=jnp.float32
            ).astype(jnp.bfloat16)
            value_rows[at, cols] = jnp.dot(
                probs.astype(jnp.bfloat16), d, preferred_element_type=jnp.float32
            ).astype(jnp.bfloat16)
        return carry

    lax.fori_loop(0, half, attend, 0)

    def part_copy(s, ls, dq):
        q = lax.rem(mq + dq, quarters)
        return pltpu.make_async_remote_copy(
            src_ref=part.at[dq - 1, s, ls],
            dst_ref=inbox.at[dq - 1, s, ls],
            send_sem=part_send.at[dq - 1, s, ls],
            recv_sem=part_recv.at[dq - 1, s, ls],
            device_id=(ms, ml, q),
            device_id_type=MESH,
        )

    def project_back(s, q, m):
        start = pl.multiple_of((s * quarters + q) * eighth, eighth)
        at = pl.ds(pl.multiple_of(m * tall, tall), tall)
        term = lax.dot_general(
            key_rows[at, :], key_w[pl.ds(start, eighth), :], NT,
            preferred_element_type=jnp.float32,
        )
        return term + lax.dot_general(
            value_rows[at, :], value_w[pl.ds(start, eighth), :], NT,
            preferred_element_type=jnp.float32,
        )

    chunks = half // pair

    def send_part(i, carry):
        m = lax.rem(i, chunks)
        s = lax.rem(lax.div(i, chunks), sectors)
        dq = quarters - 1 - lax.div(i, chunks * sectors)
        term = project_back(s, lax.rem(mq + dq, quarters), m)
        part[dq - 1, s, pl.ds(m * pair, pair)] = term.astype(jnp.bfloat16).reshape(
            pair, source, eighth
        )
        for p in range(pair):
            part_copy(s, m * pair + p, dq).start()
        return carry

    lax.fori_loop(0, (quarters - 1) * sectors * chunks, send_part, 0)

    def keep_part(i, carry):
        m, s = lax.rem(i, chunks), lax.div(i, chunks)
        own[s, pl.ds(m * pair, pair)] = project_back(s, mq, m).reshape(pair, source, eighth)
        return carry

    lax.fori_loop(0, sectors * chunks, keep_part, 0)

    def back_copy(s, ls):
        return pltpu.make_async_remote_copy(
            src_ref=reduced.at[s, ls],
            dst_ref=arrived.at[ml],
            send_sem=back_send.at[s, ls],
            recv_sem=back_recv.at[ml],
            device_id=(s, ms * half + ls, mq),
            device_id_type=MESH,
        )

    def local_back(s, ls):
        return pltpu.make_async_copy(reduced.at[s, ls], arrived.at[ml], back_recv.at[ml])

    def is_me(s, ls):
        return jnp.logical_and(s == ms, ms * half + ls == ml)

    def reduce(i, carry):
        ls, s = lax.rem(i, half), lax.div(i, half)
        total = own[s, ls]
        for dq in range(quarters - 1, 0, -1):
            view = inbox.at[dq - 1, s, ls]
            pltpu.make_async_copy(view, view, part_recv.at[dq - 1, s, ls]).wait()
            total = total + inbox[dq - 1, s, ls].astype(jnp.float32)
        reduced[s, ls] = total.astype(jnp.bfloat16)

        @pl.when(is_me(s, ls))
        def _():
            local_back(s, ls).start()

        @pl.when(jnp.logical_not(is_me(s, ls)))
        def _():
            back_copy(s, ls).start()

        return carry

    lax.fori_loop(0, sectors * half, reduce, 0)

    for g in range(groups):
        view = arrived.at[g]
        pltpu.make_async_copy(view, view, back_recv.at[g]).wait()
    for j in range(blocks):
        group = 0
        for c in range(languages):
            group = group + jnp.where(rank[c] == j, live[c] * group_of_lang[c], 0)
        out[0, j] = arrived[group]

    @pl.when(jnp.logical_not(at_home))
    def _():
        for copy in z_copy(0):
            copy.wait_send()

    for dl in range(1, groups):
        for copy in z_copy(dl):
            copy.wait_send()

    def drain(i, carry):
        ls, s = lax.rem(i, half), lax.div(i, half)
        for dq in range(1, quarters):
            mp_copy(s, ls, dq).wait_send()
            part_copy(s, ls, dq).wait_send()

        @pl.when(jnp.logical_not(is_me(s, ls)))
        def _():
            back_copy(s, ls).wait_send()

        return carry

    lax.fori_loop(0, sectors * half, drain, 0)


def body(memory, queries, out_grad, key_weight, value_weight, lang_rows, group_of_lang, src_len):
    blocks, source, eighth = memory.shape[1:]
    width, heads_w = key_weight.shape[1:]
    sectors, groups = lax.axis_size("sect"), lax.axis_size("lang")
    quarters = lax.axis_size("mp")
    half = groups // sectors
    dims = (sectors, groups, quarters, half, blocks, source, eighth, width, heads_w)
    low, full = jnp.bfloat16, jnp.float32
    vmem = pl.BlockSpec(memory_space=pltpu.VMEM)
    smem = pl.BlockSpec(memory_space=pltpu.SMEM)
    hbm = pl.BlockSpec(memory_space=pl.ANY)
    dma = pltpu.SemaphoreType.DMA
    scratch = [
        pltpu.VMEM((width, heads_w), low),
        pltpu.VMEM((width, heads_w), low),
        pltpu.VMEM(queries.shape[1:], low),
        pltpu.VMEM(queries.shape[1:], low),
        pltpu.VMEM((groups, source, eighth), low),
        pltpu.VMEM((groups, 8, queries.shape[2]), jnp.int32),
        pltpu.VMEM((half, sectors, 8, queries.shape[2]), jnp.int32),
        pltpu.VMEM((sectors, quarters, half, source, eighth), low),
        pltpu.VMEM((half * source, heads_w), full),
        pltpu.VMEM((half * source, heads_w), full),
        pltpu.VMEM((half * source, heads_w), low),
        pltpu.VMEM((half * source, heads_w), low),
        pltpu.VMEM((quarters - 1, sectors, half, source, eighth), low),
        pltpu.VMEM((sectors, half, source, eighth), full),
        pltpu.VMEM((quarters - 1, sectors, half, source, eighth), low),
        pltpu.VMEM((sectors, half, source, eighth), low),
        pltpu.VMEM((groups, source, eighth), low),
        dma((4,)),
        dma((groups,)),
        dma((groups,)),
        dma((half, sectors)),
        dma((sectors, quarters, half)),
        dma((quarters - 1, sectors, half)),
        dma((quarters - 1, sectors, half)),
        dma((quarters - 1, sectors, half)),
        dma((sectors, half)),
        dma((groups,)),
    ]
    return pl.pallas_call(
        functools.partial(kernel, dims),
        out_shape=jax.ShapeDtypeStruct(memory.shape, memory.dtype),
        in_specs=[smem, smem, smem, vmem, hbm, hbm, hbm, hbm],
        out_specs=vmem,
        scratch_shapes=scratch,
        compiler_params=pltpu.CompilerParams(
            collective_id=0, has_side_effects=True, vmem_limit_bytes=67043328
        ),
    )(lang_rows, group_of_lang, src_len, memory, queries, out_grad, key_weight, value_weight)


def solution(mesh):
    in_specs = (
        P("lang", None, None, ("sect", "mp")),
        P("lang", "sect", None, "mp"),
        P("lang", "sect", None, "mp"),
        P("lang", None, "mp"),
        P("lang", None, "mp"),
        P("lang", None),
        P(),
        P("lang", None),
    )
    out_specs = P("lang", None, None, ("sect", "mp"))
    return jax.shard_map(body, mesh=mesh, in_specs=in_specs, out_specs=out_specs, check_vma=False)
```

```python
import functools

import jax
import jax.numpy as jnp
from jax import lax
from jax.experimental import pallas as pl
from jax.experimental.pallas import tpu as pltpu
from jax.sharding import PartitionSpec as P

HD = 128
MESH = pl.DeviceIdType.MESH
NT = (((1,), (1,)), ((), ()))


def kernel(
    dims,
    lang_rows,
    group_of_lang,
    src_len,
    memory_hbm,
    queries_hbm,
    grads_hbm,
    key_hbm,
    value_hbm,
    out,
    key_w,
    value_w,
    memory,
    query_v,
    grad_v,
    outgoing,
    out_len,
    got_len,
    rows,
    acc_k,
    acc_v,
    key_rows,
    value_rows,
    part,
    own,
    inbox,
    reduced,
    arrived,
    load_sem,
    z_send,
    z_len_send,
    len_recv,
    rows_recv,
    mp_send,
    part_send,
    part_recv,
    back_send,
    back_recv,
):
    sectors, groups, quarters, half, blocks, source, eighth, width, heads_w = dims
    ms, ml, mq = lax.axis_index("sect"), lax.axis_index("lang"), lax.axis_index("mp")
    languages = lang_rows.shape[1]

    loads = [
        pltpu.make_async_copy(key_hbm.at[0], key_w, load_sem.at[0]),
        pltpu.make_async_copy(value_hbm.at[0], value_w, load_sem.at[1]),
        pltpu.make_async_copy(queries_hbm.at[0], query_v, load_sem.at[2]),
        pltpu.make_async_copy(grads_hbm.at[0], grad_v, load_sem.at[3]),
    ]

    fetch = pltpu.make_async_copy(memory_hbm, memory, load_sem.at[4])
    fetch.start()
    barrier = pltpu.get_barrier_semaphore()
    for ds in range(sectors):
        for dl in range(groups):
            if ds or dl:
                peer = (lax.rem(ms + ds, sectors), lax.rem(ml + dl, groups), mq)
                pl.semaphore_signal(barrier, inc=1, device_id=peer, device_id_type=MESH)
    for dq in range(1, quarters):
        peer = (ms, ml, lax.rem(mq + dq, quarters))
        pl.semaphore_signal(barrier, inc=1, device_id=peer, device_id_type=MESH)
    for load in loads:
        load.start()

    live, rank, count = [], [], 0
    for c in range(languages):
        live.append((lang_rows[0, c] > 0).astype(jnp.int32))
        rank.append(count)
        count = count + live[c]
    home = lax.div(ml, half)
    slot = lax.rem(ml, half)
    at_home = home == ms
    fetch.wait()
    for dl in range(groups):
        g = lax.rem(ml + dl, groups)
        index, routed = 0, 0
        for c in range(languages):
            hit = jnp.where(group_of_lang[c] == g, live[c], 0)
            index = index + hit * rank[c]
            routed = routed + hit
        outgoing[dl] = memory[0, index]
        length = jnp.maximum(jnp.where(routed > 0, src_len[0, index], 1), 1)
        out_len[dl] = jnp.full(out_len.shape[1:], length, jnp.int32)

    pl.semaphore_wait(barrier, sectors * groups - 1 + quarters - 1)

    def z_copy(dl):
        g = lax.rem(ml + dl, groups)
        data = pltpu.make_async_remote_copy(
            src_ref=outgoing.at[dl],
            dst_ref=rows.at[ms, mq, slot],
            send_sem=z_send.at[dl],
            recv_sem=rows_recv.at[ms, mq, slot],
            device_id=(home, g, mq),
            device_id_type=MESH,
        )
        lens = pltpu.make_async_remote_copy(
            src_ref=out_len.at[dl],
            dst_ref=got_len.at[slot, ms],
            send_sem=z_len_send.at[dl],
            recv_sem=len_recv.at[slot, ms],
            device_id=(home, g, mq),
            device_id_type=MESH,
        )
        return data, lens

    def local_in():
        return (
            pltpu.make_async_copy(
                outgoing.at[0], rows.at[ms, mq, slot], rows_recv.at[ms, mq, slot]
            ),
            pltpu.make_async_copy(
                out_len.at[0], got_len.at[slot, ms], len_recv.at[slot, ms]
            ),
        )

    @pl.when(at_home)
    def _():
        for copy in local_in():
            copy.start()

    @pl.when(jnp.logical_not(at_home))
    def _():
        for copy in z_copy(0):
            copy.start()

    for dl in range(1, groups):
        for copy in z_copy(dl):
            copy.start()

    relay = quarters == 4

    def peer(dq):
        if not relay:
            return lax.rem(mq + dq, quarters)
        near = mq + 1 - 2 * lax.rem(mq, 2)
        far = mq + 2 - 4 * lax.div(mq, 2)
        if isinstance(dq, int):
            return (mq, near, far, 3 - mq)[dq]
        return jnp.where(dq == 0, mq, jnp.where(dq == 1, near, jnp.where(dq == 2, far, 3 - mq)))

    def first_axis(s):
        return 1 + s % 2 if isinstance(s, int) else 1 + lax.rem(s, 2)

    def landed(s, q, ls):
        view = rows.at[s, q, ls]
        pltpu.make_async_copy(view, view, rows_recv.at[s, q, ls]).wait()

    def mp_copy(s, ls, dq):
        return pltpu.make_async_remote_copy(
            src_ref=rows.at[s, mq, ls],
            dst_ref=rows.at[s, mq, ls],
            send_sem=mp_send.at[dq - 1, s, ls],
            recv_sem=rows_recv.at[s, mq, ls],
            device_id=(ms, ml, peer(dq)),
            device_id_type=MESH,
        )

    def relay_copy(s, ls):
        q = peer(3 - first_axis(s))
        return pltpu.make_async_remote_copy(
            src_ref=rows.at[s, q, ls],
            dst_ref=rows.at[s, q, ls],
            send_sem=mp_send.at[2, s, ls],
            recv_sem=rows_recv.at[s, q, ls],
            device_id=(ms, ml, peer(first_axis(s))),
            device_id_type=MESH,
        )

    nearest = jnp.clip(ml - ms * half, 0, half - 1)

    def slot_of(k):
        return lax.rem(nearest + k, half)

    spread = (2, 1) if relay else tuple(range(quarters - 1, 0, -1))

    def gather(ls):
        for s in range(sectors):
            landed(s, mq, ls)
            for dq in spread:
                mp_copy(s, ls, dq).start()

    def pass_on(ls):
        if relay:
            for s in range(sectors):
                landed(s, peer(3 - first_axis(s)), ls)
                relay_copy(s, ls).start()

    def project(ls):
        acc_k[...] = jnp.zeros_like(acc_k)
        acc_v[...] = jnp.zeros_like(acc_v)

        def step(i, carry):
            dq, s = lax.div(i, sectors), lax.rem(i, sectors)
            q = peer(dq)
            fresh = dq > 0
            if relay:
                fresh = jnp.logical_and(fresh, dq != 3 - first_axis(s))

            @pl.when(fresh)
            def _():
                landed(s, q, ls)

            at = pl.ds(pl.multiple_of((s * quarters + q) * eighth, eighth), eighth)
            x = rows[s, q, ls]
            acc_k[...] += jnp.dot(x, key_w[at, :], preferred_element_type=jnp.float32)
            acc_v[...] += jnp.dot(x, value_w[at, :], preferred_element_type=jnp.float32)
            return carry

        lax.fori_loop(0, sectors * quarters, step, 0)

    scaling = HD ** (-0.5)
    position = lax.broadcasted_iota(jnp.int32, (source, query_v.shape[1]), 0)

    def attend(ls):
        for s in range(sectors):
            view = got_len.at[ls, s]
            pltpu.make_async_copy(view, view, len_recv.at[ls, s]).wait()
        visible = position < got_len[ls, 0][0:1, :]
        for h in range(heads_w // HD):
            cols = slice(h * HD, (h + 1) * HD)
            k = acc_k[:, cols].astype(jnp.bfloat16)
            v = acc_v[:, cols].astype(jnp.bfloat16)
            q = query_v[ls, :, cols]
            d = grad_v[ls, :, cols]
            scores = lax.dot_general(k, q, NT, preferred_element_type=jnp.float32) * scaling
            weights = jnp.where(visible, jnp.exp(scores), 0.0)
            probs = weights / jnp.sum(weights, axis=0, keepdims=True)
            grad_probs = lax.dot_general(v, d, NT, preferred_element_type=jnp.float32)
            deltas = jnp.sum(probs * grad_probs, axis=0, keepdims=True)
            grad_scores = (probs * (grad_probs - deltas) * scaling).astype(jnp.bfloat16)
            key_rows[:, cols] = jnp.dot(
                grad_scores, q, preferred_element_type=jnp.float32
            ).astype(jnp.bfloat16)
            value_rows[:, cols] = jnp.dot(
                probs.astype(jnp.bfloat16), d, preferred_element_type=jnp.float32
            ).astype(jnp.bfloat16)

    def part_copy(s, ls, dq):
        to = peer(dq)
        if relay:
            if isinstance(dq, int):
                to = peer(first_axis(s)) if dq == 3 else to
            else:
                to = jnp.where(dq == 3, peer(first_axis(s)), to)
        return pltpu.make_async_remote_copy(
            src_ref=part.at[dq - 1, s, ls],
            dst_ref=inbox.at[dq - 1, s, ls],
            send_sem=part_send.at[dq - 1, s, ls],
            recv_sem=part_recv.at[dq - 1, s, ls],
            device_id=(ms, ml, to),
            device_id_type=MESH,
        )

    def project_back(s, q):
        at = pl.ds(pl.multiple_of((s * quarters + q) * eighth, eighth), eighth)
        term = lax.dot_general(
            key_rows[...], key_w[at, :], NT, preferred_element_type=jnp.float32
        )
        return term + lax.dot_general(
            value_rows[...], value_w[at, :], NT, preferred_element_type=jnp.float32
        )

    held = 1 if relay else 0

    def backward(ls):
        def send(i, carry):
            step, s = lax.div(i, sectors), lax.rem(i, sectors)
            dq = quarters - 1 - step
            if relay:
                dq = jnp.where(step == 0, 3, first_axis(s))
            part[dq - 1, s, ls] = project_back(s, peer(dq)).astype(jnp.bfloat16)
            part_copy(s, ls, dq).start()
            return carry

        lax.fori_loop(0, sectors * (quarters - 1 - held), send, 0)

        def keep(i, carry):
            step, s = lax.div(i, sectors), lax.rem(i, sectors)
            dq = jnp.where(step == 0, 3 - first_axis(s), 0) if relay else 0
            own[held - step, s, ls] = project_back(s, peer(dq))
            return carry

        lax.fori_loop(0, sectors * (1 + held), keep, 0)

    def part_landed(s, ls, dq):
        view = inbox.at[dq - 1, s, ls]
        pltpu.make_async_copy(view, view, part_recv.at[dq - 1, s, ls]).wait()
        return inbox[dq - 1, s, ls].astype(jnp.float32)

    def sum_on(ls):
        if relay:
            for s in range(sectors):
                dq = 3 - first_axis(s)
                total = own[1, s, ls] + part_landed(s, ls, 3)
                part[dq - 1, s, ls] = total.astype(jnp.bfloat16)
                part_copy(s, ls, dq).start()

    def back_copy(s, ls):
        return pltpu.make_async_remote_copy(
            src_ref=reduced.at[s, ls],
            dst_ref=arrived.at[ml],
            send_sem=back_send.at[s, ls],
            recv_sem=back_recv.at[ml],
            device_id=(s, ms * half + ls, mq),
            device_id_type=MESH,
        )

    def local_back(s, ls):
        return pltpu.make_async_copy(reduced.at[s, ls], arrived.at[ml], back_recv.at[ml])

    def is_me(s, ls):
        return jnp.logical_and(s == ms, ms * half + ls == ml)

    def give_back(ls):
        for s in range(sectors):
            total = own[0, s, ls]
            if relay:
                total = total + part_landed(s, ls, first_axis(s))
                total = total + part_landed(s, ls, 3 - first_axis(s))
            else:
                for dq in range(1, quarters):
                    total = total + part_landed(s, ls, dq)
            reduced[s, ls] = total.astype(jnp.bfloat16)

            @pl.when(is_me(s, ls))
            def _():
                local_back(s, ls).start()

            @pl.when(jnp.logical_not(is_me(s, ls)))
            def _():
                back_copy(s, ls).start()

    gather(slot_of(0))
    pass_on(slot_of(0))
    for k in range(half):
        if k + 1 < half:
            gather(slot_of(k + 1))
        if k == 0:
            for load in loads:
                load.wait()
        project(slot_of(k))
        if k + 1 < half:
            pass_on(slot_of(k + 1))
        attend(slot_of(k))
        if k > 0:
            sum_on(slot_of(k - 1))
        backward(slot_of(k))
        if k > 0:
            give_back(slot_of(k - 1))
    sum_on(slot_of(half - 1))
    give_back(slot_of(half - 1))

    for g in range(groups):
        view = arrived.at[g]
        pltpu.make_async_copy(view, view, back_recv.at[g]).wait()
    for j in range(blocks):
        group = 0
        for c in range(languages):
            group = group + jnp.where(rank[c] == j, live[c] * group_of_lang[c], 0)
        out[0, j] = arrived[group]

    @pl.when(jnp.logical_not(at_home))
    def _():
        for copy in z_copy(0):
            copy.wait_send()

    for dl in range(1, groups):
        for copy in z_copy(dl):
            copy.wait_send()

    def drain(i, carry):
        ls, s = lax.rem(i, half), lax.div(i, half)
        for dq in range(1, quarters):
            mp_copy(s, ls, dq).wait_send()
            part_copy(s, ls, dq).wait_send()

        @pl.when(jnp.logical_not(is_me(s, ls)))
        def _():
            back_copy(s, ls).wait_send()

        return carry

    lax.fori_loop(0, sectors * half, drain, 0)


def body(memory, queries, out_grad, key_weight, value_weight, lang_rows, group_of_lang, src_len):
    blocks, source, eighth = memory.shape[1:]
    width, heads_w = key_weight.shape[1:]
    sectors, groups = lax.axis_size("sect"), lax.axis_size("lang")
    quarters = lax.axis_size("mp")
    half = groups // sectors
    dims = (sectors, groups, quarters, half, blocks, source, eighth, width, heads_w)
    low, full = jnp.bfloat16, jnp.float32
    vmem = pl.BlockSpec(memory_space=pltpu.VMEM)
    smem = pl.BlockSpec(memory_space=pltpu.SMEM)
    hbm = pl.BlockSpec(memory_space=pl.ANY)
    dma = pltpu.SemaphoreType.DMA
    scratch = [
        pltpu.VMEM((width, heads_w), low),
        pltpu.VMEM((width, heads_w), low),
        pltpu.VMEM(memory.shape, low),
        pltpu.VMEM(queries.shape[1:], low),
        pltpu.VMEM(queries.shape[1:], low),
        pltpu.VMEM((groups, source, eighth), low),
        pltpu.VMEM((groups, 8, queries.shape[2]), jnp.int32),
        pltpu.VMEM((half, sectors, 8, queries.shape[2]), jnp.int32),
        pltpu.VMEM((sectors, quarters, half, source, eighth), low),
        pltpu.VMEM((source, heads_w), full),
        pltpu.VMEM((source, heads_w), full),
        pltpu.VMEM((source, heads_w), low),
        pltpu.VMEM((source, heads_w), low),
        pltpu.VMEM((quarters - 1, sectors, half, source, eighth), low),
        pltpu.VMEM((2, sectors, half, source, eighth), full),
        pltpu.VMEM((quarters - 1, sectors, half, source, eighth), low),
        pltpu.VMEM((sectors, half, source, eighth), low),
        pltpu.VMEM((groups, source, eighth), low),
        dma((5,)),
        dma((groups,)),
        dma((groups,)),
        dma((half, sectors)),
        dma((sectors, quarters, half)),
        dma((quarters - 1, sectors, half)),
        dma((quarters - 1, sectors, half)),
        dma((quarters - 1, sectors, half)),
        dma((sectors, half)),
        dma((groups,)),
    ]
    return pl.pallas_call(
        functools.partial(kernel, dims),
        out_shape=jax.ShapeDtypeStruct(memory.shape, memory.dtype),
        in_specs=[smem, smem, smem, hbm, hbm, hbm, hbm, hbm],
        out_specs=vmem,
        scratch_shapes=scratch,
        compiler_params=pltpu.CompilerParams(
            collective_id=0, has_side_effects=True, vmem_limit_bytes=67043328
        ),
    )(lang_rows, group_of_lang, src_len, memory, queries, out_grad, key_weight, value_weight)


def solution(mesh):
    in_specs = (
        P("lang", None, None, ("sect", "mp")),
        P("lang", "sect", None, "mp"),
        P("lang", "sect", None, "mp"),
        P("lang", None, "mp"),
        P("lang", None, "mp"),
        P("lang", None),
        P(),
        P("lang", None),
    )
    out_specs = P("lang", None, None, ("sect", "mp"))
    return jax.shard_map(body, mesh=mesh, in_specs=in_specs, out_specs=out_specs, check_vma=False)
```

```python
import functools

import jax
import jax.numpy as jnp
from jax import lax
from jax.experimental import pallas as pl
from jax.experimental.pallas import tpu as pltpu
from jax.sharding import PartitionSpec as P

HD = 128
MESH = pl.DeviceIdType.MESH
NT = (((1,), (1,)), ((), ()))


def kernel(
    dims,
    lang_rows,
    group_of_lang,
    src_len,
    memory_hbm,
    queries_hbm,
    grads_hbm,
    key_hbm,
    value_hbm,
    out,
    key_w,
    value_w,
    memory,
    query_v,
    grad_v,
    outgoing,
    out_len,
    got_len,
    rows,
    acc_k,
    acc_v,
    key_rows,
    value_rows,
    part,
    own,
    inbox,
    reduced,
    arrived,
    load_sem,
    z_send,
    z_len_send,
    len_recv,
    rows_recv,
    mp_send,
    part_send,
    part_recv,
    back_send,
    back_recv,
):
    sectors, groups, quarters, half, blocks, source, eighth, width, heads_w = dims
    ms, ml, mq = lax.axis_index("sect"), lax.axis_index("lang"), lax.axis_index("mp")
    languages = lang_rows.shape[1]

    loads = [
        pltpu.make_async_copy(key_hbm.at[0], key_w, load_sem.at[0]),
        pltpu.make_async_copy(value_hbm.at[0], value_w, load_sem.at[1]),
        pltpu.make_async_copy(queries_hbm.at[0], query_v, load_sem.at[2]),
        pltpu.make_async_copy(grads_hbm.at[0], grad_v, load_sem.at[3]),
    ]

    fetch = pltpu.make_async_copy(memory_hbm, memory, load_sem.at[4])
    fetch.start()
    barrier = pltpu.get_barrier_semaphore()
    for ds in range(sectors):
        for dl in range(groups):
            if ds or dl:
                peer = (lax.rem(ms + ds, sectors), lax.rem(ml + dl, groups), mq)
                pl.semaphore_signal(barrier, inc=1, device_id=peer, device_id_type=MESH)
    for dq in range(1, quarters):
        peer = (ms, ml, lax.rem(mq + dq, quarters))
        pl.semaphore_signal(barrier, inc=1, device_id=peer, device_id_type=MESH)
    for load in loads:
        load.start()

    live, rank, count = [], [], 0
    for c in range(languages):
        live.append((lang_rows[0, c] > 0).astype(jnp.int32))
        rank.append(count)
        count = count + live[c]
    home = lax.div(ml, half)
    slot = lax.rem(ml, half)
    at_home = home == ms
    fetch.wait()
    for dl in range(groups):
        g = lax.rem(ml + dl, groups)
        index, routed = 0, 0
        for c in range(languages):
            hit = jnp.where(group_of_lang[c] == g, live[c], 0)
            index = index + hit * rank[c]
            routed = routed + hit
        outgoing[dl] = memory[0, index]
        length = jnp.maximum(jnp.where(routed > 0, src_len[0, index], 1), 1)
        out_len[dl] = jnp.full(out_len.shape[1:], length, jnp.int32)

    pl.semaphore_wait(barrier, sectors * groups - 1 + quarters - 1)

    def z_copy(dl):
        g = lax.rem(ml + dl, groups)
        data = pltpu.make_async_remote_copy(
            src_ref=outgoing.at[dl],
            dst_ref=rows.at[ms, mq, slot],
            send_sem=z_send.at[dl],
            recv_sem=rows_recv.at[ms, mq, slot],
            device_id=(home, g, mq),
            device_id_type=MESH,
        )
        lens = pltpu.make_async_remote_copy(
            src_ref=out_len.at[dl],
            dst_ref=got_len.at[slot, ms],
            send_sem=z_len_send.at[dl],
            recv_sem=len_recv.at[slot, ms],
            device_id=(home, g, mq),
            device_id_type=MESH,
        )
        return data, lens

    def local_in():
        return (
            pltpu.make_async_copy(
                outgoing.at[0], rows.at[ms, mq, slot], rows_recv.at[ms, mq, slot]
            ),
            pltpu.make_async_copy(
                out_len.at[0], got_len.at[slot, ms], len_recv.at[slot, ms]
            ),
        )

    @pl.when(at_home)
    def _():
        for copy in local_in():
            copy.start()

    @pl.when(jnp.logical_not(at_home))
    def _():
        for copy in z_copy(0):
            copy.start()

    for dl in range(1, groups):
        for copy in z_copy(dl):
            copy.start()

    relay = quarters == 4

    def peer(dq):
        if not relay:
            return lax.rem(mq + dq, quarters)
        near = mq + 1 - 2 * lax.rem(mq, 2)
        far = mq + 2 - 4 * lax.div(mq, 2)
        if isinstance(dq, int):
            return (mq, near, far, 3 - mq)[dq]
        return jnp.where(dq == 0, mq, jnp.where(dq == 1, near, jnp.where(dq == 2, far, 3 - mq)))

    def first_axis(s):
        return 1 + s % 2 if isinstance(s, int) else 1 + lax.rem(s, 2)

    def landed(s, q, ls):
        view = rows.at[s, q, ls]
        pltpu.make_async_copy(view, view, rows_recv.at[s, q, ls]).wait()

    def mp_copy(s, ls, dq):
        return pltpu.make_async_remote_copy(
            src_ref=rows.at[s, mq, ls],
            dst_ref=rows.at[s, mq, ls],
            send_sem=mp_send.at[dq - 1, s, ls],
            recv_sem=rows_recv.at[s, mq, ls],
            device_id=(ms, ml, peer(dq)),
            device_id_type=MESH,
        )

    def relay_copy(s, ls):
        q = peer(3 - first_axis(s))
        return pltpu.make_async_remote_copy(
            src_ref=rows.at[s, q, ls],
            dst_ref=rows.at[s, q, ls],
            send_sem=mp_send.at[2, s, ls],
            recv_sem=rows_recv.at[s, q, ls],
            device_id=(ms, ml, peer(first_axis(s))),
            device_id_type=MESH,
        )

    nearest = jnp.clip(ml - ms * half, 0, half - 1)

    def slot_of(k):
        return lax.rem(nearest + k, half)

    spread = (2, 1) if relay else tuple(range(quarters - 1, 0, -1))

    def gather(ls, s):
        landed(s, mq, ls)
        for dq in spread:
            mp_copy(s, ls, dq).start()

    def pass_on(ls, s):
        if relay:
            landed(s, peer(3 - first_axis(s)), ls)
            relay_copy(s, ls).start()

    def project(ls):
        acc_k[...] = jnp.zeros_like(acc_k)
        acc_v[...] = jnp.zeros_like(acc_v)

        def step(i, carry):
            dq, s = lax.div(i, sectors), lax.rem(i, sectors)
            q = peer(dq)
            fresh = dq > 0
            if relay:
                fresh = jnp.logical_and(fresh, dq != 3 - first_axis(s))

            @pl.when(fresh)
            def _():
                landed(s, q, ls)

            at = pl.ds(pl.multiple_of((s * quarters + q) * eighth, eighth), eighth)
            x = rows[s, q, ls]
            acc_k[...] += jnp.dot(x, key_w[at, :], preferred_element_type=jnp.float32)
            acc_v[...] += jnp.dot(x, value_w[at, :], preferred_element_type=jnp.float32)
            return carry

        lax.fori_loop(0, sectors * quarters, step, 0)

    scaling = HD ** (-0.5)
    position = lax.broadcasted_iota(jnp.int32, (source, query_v.shape[1]), 0)

    def attend(ls):
        for s in range(sectors):
            view = got_len.at[ls, s]
            pltpu.make_async_copy(view, view, len_recv.at[ls, s]).wait()
        visible = position < got_len[ls, 0][0:1, :]
        for h in range(heads_w // HD):
            cols = slice(h * HD, (h + 1) * HD)
            k = acc_k[:, cols].astype(jnp.bfloat16)
            v = acc_v[:, cols].astype(jnp.bfloat16)
            q = query_v[ls, :, cols]
            d = grad_v[ls, :, cols]
            scores = lax.dot_general(k, q, NT, preferred_element_type=jnp.float32) * scaling
            weights = jnp.where(visible, jnp.exp(scores), 0.0)
            probs = weights / jnp.sum(weights, axis=0, keepdims=True)
            grad_probs = lax.dot_general(v, d, NT, preferred_element_type=jnp.float32)
            deltas = jnp.sum(probs * grad_probs, axis=0, keepdims=True)
            grad_scores = (probs * (grad_probs - deltas) * scaling).astype(jnp.bfloat16)
            key_rows[:, cols] = jnp.dot(
                grad_scores, q, preferred_element_type=jnp.float32
            ).astype(jnp.bfloat16)
            value_rows[:, cols] = jnp.dot(
                probs.astype(jnp.bfloat16), d, preferred_element_type=jnp.float32
            ).astype(jnp.bfloat16)

    def part_copy(s, ls, dq):
        to = peer(dq)
        if relay:
            if isinstance(dq, int):
                to = peer(first_axis(s)) if dq == 3 else to
            else:
                to = jnp.where(dq == 3, peer(first_axis(s)), to)
        return pltpu.make_async_remote_copy(
            src_ref=part.at[dq - 1, s, ls],
            dst_ref=inbox.at[dq - 1, s, ls],
            send_sem=part_send.at[dq - 1, s, ls],
            recv_sem=part_recv.at[dq - 1, s, ls],
            device_id=(ms, ml, to),
            device_id_type=MESH,
        )

    def project_back(s, q):
        at = pl.ds(pl.multiple_of((s * quarters + q) * eighth, eighth), eighth)
        term = lax.dot_general(
            key_rows[...], key_w[at, :], NT, preferred_element_type=jnp.float32
        )
        return term + lax.dot_general(
            value_rows[...], value_w[at, :], NT, preferred_element_type=jnp.float32
        )

    held = 1 if relay else 0

    def backward(ls):
        def send(i, carry):
            step, s = lax.div(i, sectors), lax.rem(i, sectors)
            dq = quarters - 1 - step
            if relay:
                dq = jnp.where(step == 0, 3, first_axis(s))
            part[dq - 1, s, ls] = project_back(s, peer(dq)).astype(jnp.bfloat16)
            part_copy(s, ls, dq).start()
            return carry

        lax.fori_loop(0, sectors * (quarters - 1 - held), send, 0)

        def keep(i, carry):
            step, s = lax.div(i, sectors), lax.rem(i, sectors)
            dq = jnp.where(step == 0, 3 - first_axis(s), 0) if relay else 0
            own[held - step, s, ls] = project_back(s, peer(dq))
            return carry

        lax.fori_loop(0, sectors * (1 + held), keep, 0)

    def part_landed(s, ls, dq):
        view = inbox.at[dq - 1, s, ls]
        pltpu.make_async_copy(view, view, part_recv.at[dq - 1, s, ls]).wait()
        return inbox[dq - 1, s, ls].astype(jnp.float32)

    def sum_on(ls):
        if relay:
            for s in range(sectors):
                dq = 3 - first_axis(s)
                total = own[1, s, ls] + part_landed(s, ls, 3)
                part[dq - 1, s, ls] = total.astype(jnp.bfloat16)
                part_copy(s, ls, dq).start()

    def back_copy(s, ls):
        return pltpu.make_async_remote_copy(
            src_ref=reduced.at[s, ls],
            dst_ref=arrived.at[ml],
            send_sem=back_send.at[s, ls],
            recv_sem=back_recv.at[ml],
            device_id=(s, ms * half + ls, mq),
            device_id_type=MESH,
        )

    def local_back(s, ls):
        return pltpu.make_async_copy(reduced.at[s, ls], arrived.at[ml], back_recv.at[ml])

    def is_me(s, ls):
        return jnp.logical_and(s == ms, ms * half + ls == ml)

    def give_back(ls):
        for s in range(sectors):
            total = own[0, s, ls]
            if relay:
                total = total + part_landed(s, ls, first_axis(s))
                total = total + part_landed(s, ls, 3 - first_axis(s))
            else:
                for dq in range(1, quarters):
                    total = total + part_landed(s, ls, dq)
            reduced[s, ls] = total.astype(jnp.bfloat16)

            @pl.when(is_me(s, ls))
            def _():
                local_back(s, ls).start()

            @pl.when(jnp.logical_not(is_me(s, ls)))
            def _():
                back_copy(s, ls).start()

    for s in range(sectors):
        gather(slot_of(0), s)
    for k in range(half):
        for s in range(sectors):
            if k == 0:
                pass_on(slot_of(k), s)
            if k + 1 < half:
                gather(slot_of(k + 1), s)
        if k == 0:
            for load in loads:
                load.wait()
        project(slot_of(k))
        attend(slot_of(k))
        if k + 1 < half:
            for s in range(sectors):
                pass_on(slot_of(k + 1), s)
        if k > 0:
            sum_on(slot_of(k - 1))
        backward(slot_of(k))
        if k > 0:
            give_back(slot_of(k - 1))
    sum_on(slot_of(half - 1))
    give_back(slot_of(half - 1))

    for g in range(groups):
        view = arrived.at[g]
        pltpu.make_async_copy(view, view, back_recv.at[g]).wait()
    for j in range(blocks):
        group = 0
        for c in range(languages):
            group = group + jnp.where(rank[c] == j, live[c] * group_of_lang[c], 0)
        out[0, j] = arrived[group]

    @pl.when(jnp.logical_not(at_home))
    def _():
        for copy in z_copy(0):
            copy.wait_send()

    for dl in range(1, groups):
        for copy in z_copy(dl):
            copy.wait_send()

    def drain(i, carry):
        ls, s = lax.rem(i, half), lax.div(i, half)
        for dq in range(1, quarters):
            mp_copy(s, ls, dq).wait_send()
            part_copy(s, ls, dq).wait_send()

        @pl.when(jnp.logical_not(is_me(s, ls)))
        def _():
            back_copy(s, ls).wait_send()

        return carry

    lax.fori_loop(0, sectors * half, drain, 0)


def body(memory, queries, out_grad, key_weight, value_weight, lang_rows, group_of_lang, src_len):
    blocks, source, eighth = memory.shape[1:]
    width, heads_w = key_weight.shape[1:]
    sectors, groups = lax.axis_size("sect"), lax.axis_size("lang")
    quarters = lax.axis_size("mp")
    half = groups // sectors
    dims = (sectors, groups, quarters, half, blocks, source, eighth, width, heads_w)
    low, full = jnp.bfloat16, jnp.float32
    vmem = pl.BlockSpec(memory_space=pltpu.VMEM)
    smem = pl.BlockSpec(memory_space=pltpu.SMEM)
    hbm = pl.BlockSpec(memory_space=pl.ANY)
    dma = pltpu.SemaphoreType.DMA
    scratch = [
        pltpu.VMEM((width, heads_w), low),
        pltpu.VMEM((width, heads_w), low),
        pltpu.VMEM(memory.shape, low),
        pltpu.VMEM(queries.shape[1:], low),
        pltpu.VMEM(queries.shape[1:], low),
        pltpu.VMEM((groups, source, eighth), low),
        pltpu.VMEM((groups, 8, queries.shape[2]), jnp.int32),
        pltpu.VMEM((half, sectors, 8, queries.shape[2]), jnp.int32),
        pltpu.VMEM((sectors, quarters, half, source, eighth), low),
        pltpu.VMEM((source, heads_w), full),
        pltpu.VMEM((source, heads_w), full),
        pltpu.VMEM((source, heads_w), low),
        pltpu.VMEM((source, heads_w), low),
        pltpu.VMEM((quarters - 1, sectors, half, source, eighth), low),
        pltpu.VMEM((2, sectors, half, source, eighth), full),
        pltpu.VMEM((quarters - 1, sectors, half, source, eighth), low),
        pltpu.VMEM((sectors, half, source, eighth), low),
        pltpu.VMEM((groups, source, eighth), low),
        dma((5,)),
        dma((groups,)),
        dma((groups,)),
        dma((half, sectors)),
        dma((sectors, quarters, half)),
        dma((quarters - 1, sectors, half)),
        dma((quarters - 1, sectors, half)),
        dma((quarters - 1, sectors, half)),
        dma((sectors, half)),
        dma((groups,)),
    ]
    return pl.pallas_call(
        functools.partial(kernel, dims),
        out_shape=jax.ShapeDtypeStruct(memory.shape, memory.dtype),
        in_specs=[smem, smem, smem, hbm, hbm, hbm, hbm, hbm],
        out_specs=vmem,
        scratch_shapes=scratch,
        compiler_params=pltpu.CompilerParams(
            collective_id=0, has_side_effects=True, vmem_limit_bytes=67043328
        ),
    )(lang_rows, group_of_lang, src_len, memory, queries, out_grad, key_weight, value_weight)


def solution(mesh):
    in_specs = (
        P("lang", None, None, ("sect", "mp")),
        P("lang", "sect", None, "mp"),
        P("lang", "sect", None, "mp"),
        P("lang", None, "mp"),
        P("lang", None, "mp"),
        P("lang", None),
        P(),
        P("lang", None),
    )
    out_specs = P("lang", None, None, ("sect", "mp"))
    return jax.shard_map(body, mesh=mesh, in_specs=in_specs, out_specs=out_specs, check_vma=False)
```
